1024 devices in a mesh: blk: 256 (over z, x, core), node: 4 (over y).
Axes of the slice: x: 4, y: 4, z: 32, core: 2. Of those that a mesh axis runs over, the one named last changes fastest.
Arguments:
- image_embeds: bfloat16 [163840, 1152], P(('blk', 'node')), may hold values from -0.1796875 to 0.1796875
- text_embeds: bfloat16 [163840, 1152], P(('blk', 'node')), may hold values from -0.1796875 to 0.1796875
- pair_text: int32 [163840], replicated, may hold values from 0 to 163839, as said below
- similarity_scale: float32 [1], replicated, may hold values from 5 to 15
- logit_bias: float32 [1], replicated, may hold values from -6 to -2
Outputs:
- image_grads: float32 [163840, 1152], P(('blk', 'node'))
- text_grads: float32 [163840, 1152], P(('blk', 'node'))
The draws below stay inside these ranges and needn't reach their ends.
Inputs may be any that keep to these rules, and one draw needn't show every extreme that they name: pair_text is a permutation that maps each image to a report of its own group of 640 consecutive pairs.
All inputs are finite; a program needn't handle non-finite values.
Results may differ from the reference program's by a relative error of at most 0.0043.
Values may be sent and summed in bfloat16 or wider, within the bound.
A program may use at most 32 MiB of HBM per device.

```python
import math
import jax
import jax.numpy as jnp
from jax import lax

D = 1152
TURNS = 3
GROUP = 640
PAIRS = 163840


def group_order(key):
    return jax.random.permutation(key, GROUP).astype(jnp.int32)


def draw_pair_text(key, part):
    group_count = PAIRS // GROUP
    keys = jax.random.split(jax.random.fold_in(key, 17), group_count)
    orders = jax.vmap(group_order)(keys)
    offsets = jnp.arange(group_count, dtype=jnp.int32)[:, None] * GROUP
    return (orders + offsets).reshape(PAIRS).astype(jnp.int32)


def level_of(rng, extent, pieces, least, high):
    def one(axis_at, parts):
        heights = jax.random.uniform(jax.random.fold_in(jax.random.fold_in(rng, 6), axis_at), (parts,), jnp.float32, least / len(pieces), high / len(pieces))
        return jnp.repeat(jnp.exp(heights), extent[axis_at] // parts).reshape((-1,) + (1,) * (len(extent) - axis_at - 1))

    level = one(*pieces[0])
    for cut in pieces[1:]:
        level = level * one(*cut)
    return level


def gaussian(own_key, shape, scale, most, cuts=(), kind=jnp.bfloat16):
    factor_of = level_of(own_key, shape, cuts, -0.22, 0.18) if cuts else 1.0
    result = jax.random.normal(own_key, shape, jnp.float32) * scale * factor_of
    return jnp.minimum(jnp.maximum(result, -most), most).astype(kind)


def setup_inputs(seed: int = 0) -> dict:
    streams_of = jax.random.split(jax.random.key(seed), 6)
    image_embeds = gaussian(streams_of[0], (PAIRS, D), 0.03, 0.1796875, ((0, 1024),))
    text_embeds = gaussian(streams_of[1], (PAIRS, D), 0.03, 0.1796875, ((0, 1024),))
    pair_text = draw_pair_text(jax.random.fold_in(streams_of[5], 71), 0)
    similarity_scale = jnp.clip(jnp.exp(jax.random.uniform(streams_of[3], (1,), jnp.float32, math.log(5.0), math.log(15.0))), 5.0, 15.0)
    logit_bias = jnp.clip(jax.random.uniform(streams_of[4], (1,), jnp.float32, -6.0, -2.0), -6.0, -2.0)
    return {"image_embeds": image_embeds, "text_embeds": text_embeds, "pair_text": pair_text, "similarity_scale": similarity_scale, "logit_bias": logit_bias}


def unit_rows(raw_rows):
    values = raw_rows.astype(jnp.float32)
    inverse = lax.rsqrt(lax.optimization_barrier(jnp.sum(values * values, axis=1, keepdims=True)) + 1e-06)
    return (values * inverse, inverse)

def tangent_part(gradient, unit_rows_f, inverse):
    return (gradient - unit_rows_f * lax.optimization_barrier(jnp.sum(unit_rows_f * gradient, axis=1, keepdims=True))) * inverse

def reference(image_embeds, text_embeds, pair_text, similarity_scale, logit_bias):
    image_unit, image_inv = unit_rows(image_embeds)
    text_unit, text_inv = unit_rows(text_embeds)
    image_half = image_unit.astype(jnp.bfloat16)
    text_half = text_unit.astype(jnp.bfloat16)
    softness_factor = similarity_scale[0]
    shift_amount_value = logit_bias[0]
    group_count = PAIRS // GROUP
    columns = jnp.arange(GROUP, dtype=jnp.int32)

    def one_group(text_total, group_index):
        row_start = (group_index * GROUP).astype(jnp.int32)
        picture_row_block = lax.dynamic_slice_in_dim(image_half, row_start, GROUP, 0)
        targets = lax.dynamic_slice_in_dim(pair_text, row_start, GROUP, 0)
        image_dir = jnp.zeros((GROUP, D), jnp.float32)
        for turn in range(TURNS):
            text_start = ((group_index + turn) % group_count * GROUP).astype(jnp.int32)
            report_vectors = lax.dynamic_slice_in_dim(text_half, text_start, GROUP, 0)
            pair_logit_matrix = softness_factor * jnp.dot(picture_row_block, report_vectors.T, preferred_element_type=jnp.float32) + shift_amount_value
            pair_label_polarity = jnp.where(targets[:, None] == (text_start + columns)[None, :], 1.0, -1.0).astype(jnp.float32)
            weight_panel = (-pair_label_polarity * softness_factor * jax.nn.sigmoid(-pair_label_polarity * pair_logit_matrix)).astype(jnp.bfloat16)
            image_dir = image_dir + jnp.dot(weight_panel, report_vectors, preferred_element_type=jnp.float32)
            previous = lax.dynamic_slice_in_dim(text_total, text_start, GROUP, 0)
            updated = previous + jnp.dot(weight_panel.T, picture_row_block, preferred_element_type=jnp.float32)
            text_total = lax.dynamic_update_slice_in_dim(text_total, updated, text_start, 0)
        return (text_total, image_dir)
    text_dir, image_parts = lax.scan(one_group, jnp.zeros((PAIRS, D), jnp.float32), jnp.arange(group_count, dtype=jnp.int32))
    image_dir = image_parts.reshape(PAIRS, D)
    image_grads = tangent_part(image_dir, image_unit, image_inv)
    text_grads = tangent_part(text_dir, text_unit, text_inv)
    return (image_grads, text_grads)
```

```python
import functools

import jax
import jax.numpy as jnp
from jax import lax
from jax.experimental import pallas as pl
from jax.experimental.pallas import tpu as pltpu
from jax.sharding import PartitionSpec as P

MESH = pl.DeviceIdType.MESH
CHUNKS = 2
GA, GB, GS, GX, GSF, GXF, RXP, RXO, RSP, RSO, RA_, RB_ = range(12)


def kernel(
    image_ref, text_ref, pair_ref, scale_ref, bias_ref,
    image_out, text_out,
    raw, held, ret_x, ret_s, ret_a, ret_b, got_x, got_s, got_a, got_b,
    total, inverse, pairs, scalars,
    send_sem, recv_sem, local_sem,
):
    rows, width = image_ref.shape
    part = rows // CHUNKS
    blk_count = lax.axis_size("blk")
    node_count = lax.axis_size("node")
    me = lax.axis_index("blk")
    y = lax.axis_index("node")
    core = lax.rem(me, 2)
    own = lax.rem(y, 2)
    other = 1 - own
    mate_a = y + 1 - 2 * own
    mate_b = lax.rem(y + node_count - 1 + 2 * own, node_count)
    sibling = me + 1 - 2 * core
    x_to = lax.rem(me + 4 * core - 2 + blk_count, blk_count)
    x_from = lax.rem(me - 4 * core + 2 + blk_count, blk_count)
    dev_a = (me, mate_a)
    dev_b = (me, mate_b)
    dev_s = (sibling, y)
    dev_to = (x_to, y)
    dev_from = (x_from, y)

    barrier = pltpu.get_barrier_semaphore()
    for peer in (dev_a, dev_b, dev_s, dev_to, dev_from):
        pl.semaphore_signal(barrier, inc=1, device_id=peer, device_id_type=MESH)

    load_image = pltpu.make_async_copy(image_ref, raw.at[0], local_sem.at[0])
    load_text = pltpu.make_async_copy(text_ref, raw.at[1], local_sem.at[1])
    load_pairs = pltpu.make_async_copy(
        pair_ref.at[pl.ds(pl.multiple_of(me * (rows * 4), 128), rows * 4)], pairs, local_sem.at[2]
    )
    load_scale = pltpu.make_async_copy(scale_ref, scalars.at[0], local_sem.at[3])
    load_bias = pltpu.make_async_copy(bias_ref, scalars.at[1], local_sem.at[4])
    for load in (load_image, load_text, load_pairs, load_scale, load_bias):
        load.start()

    def normalise(which):
        for k in range(5):
            at = pl.ds(k * (rows // 5), rows // 5)
            values = raw[which, at, :].astype(jnp.float32)
            inv = lax.rsqrt(jnp.sum(values * values, axis=1, keepdims=True) + 1e-06)
            inverse[which, at, :] = jnp.broadcast_to(inv, (rows // 5, 128))
            held[which, own, at, :] = (values * inv).astype(jnp.bfloat16)

    load_image.wait()
    normalise(0)
    load_text.wait()
    normalise(1)

    pl.semaphore_wait(barrier, 5)

    def remote(kind, k, src, dst, device):
        at = pl.ds(k * part, part)
        return pltpu.make_async_remote_copy(
            src_ref=src.at[at, :],
            dst_ref=dst.at[at, :],
            send_sem=send_sem.at[kind * CHUNKS + k],
            recv_sem=recv_sem.at[kind * CHUNKS + k],
            device_id=device,
            device_id_type=MESH,
        )

    def ga(k, slot):
        return remote(GA, k, held.at[0, slot], held.at[0, slot], dev_a)

    def gb(k, slot):
        return remote(GB, k, held.at[1, slot], held.at[1, slot], dev_b)

    def gs(k, slot, kind=GS):
        return remote(kind, k, held.at[1, slot], held.at[2, slot], dev_s)

    def gx(k, slot, kind=GX):
        return remote(kind, k, held.at[1 - core, slot], held.at[3, slot], dev_to)

    for k in range(CHUNKS):
        ga(k, own).start()
        gb(k, own).start()
        gx(k, own).start()
        gs(k, own).start()

    load_pairs.wait()
    load_scale.wait()
    load_bias.wait()
    scale = scalars[0, 0, 0]
    bias = scalars[1, 0, 0]

    for k in range(CHUNKS):
        gb(k, own).wait_recv()
        gs(k, other, GSF).start()

        @pl.when(core == 0)
        def _():
            gx(k, other, GXF).start()

        ga(k, own).wait_recv()

        @pl.when(core == 1)
        def _():
            gx(k, other, GXF).start()

    def both(ref):
        return ref[...].reshape(2 * rows, width)

    def weights_of(texts, images, positive=None):
        logits = scale * lax.dot_general(
            texts, images, (((1,), (1,)), ((), ())), preferred_element_type=jnp.float32
        ) + bias
        if positive is None:
            return (scale * jax.nn.sigmoid(logits)).astype(jnp.bfloat16)
        sign = jnp.where(positive, 1.0, -1.0)
        return (-sign * scale * jax.nn.sigmoid(-sign * logits)).astype(jnp.bfloat16)

    def to_texts(weights, images):
        return jnp.dot(weights, images, preferred_element_type=jnp.float32)

    def to_images(weights, texts):
        return lax.dot_general(
            weights, texts, (((0,), (0,)), ((), ())), preferred_element_type=jnp.float32
        )

    wide = pairs[...].reshape(1, 4 * rows) - me * (4 * rows)
    target = jnp.where(y < 2, wide[:, : 2 * rows], wide[:, 2 * rows :])
    even_y = jnp.where(own == 0, y, mate_b)
    odd_y = jnp.where(own == 0, mate_b, y)
    row_id = lax.broadcasted_iota(jnp.int32, (2 * rows, 1), 0)
    text_id = jnp.where(row_id < rows, row_id + even_y * rows, row_id - rows + odd_y * rows)
    positive = text_id == target

    weights = weights_of(both(held.at[1]), both(held.at[0]), positive)
    total[2] = to_texts(weights, both(held.at[0]))
    total[0] = to_images(weights, both(held.at[1]))

    for k in range(CHUNKS):
        gs(k, own).wait_recv()
        gs(k, own, GSF).wait_recv()

    @pl.when(core == 1)
    def _():
        total[1] = jnp.zeros_like(total[1])
        for k in range(CHUNKS):
            gx(k, own).wait_recv()
            gx(k, own, GXF).wait_recv()

    hub = held.at[3 * core]
    weights = weights_of(both(held.at[2]), both(hub))
    terms = to_texts(weights, both(hub)).astype(jnp.bfloat16)
    ret_s[...] = terms.reshape(2, rows, width)

    def rs(k, slot, kind):
        return remote(kind, k, ret_s.at[slot], got_s.at[slot], dev_s)

    for k in range(CHUNKS):
        rs(k, other, RSP).start()
    for k in range(CHUNKS):
        rs(k, own, RSO).start()
    total[core] += to_images(weights, both(held.at[2]))

    @pl.when(core == 0)
    def _():
        for k in range(CHUNKS):
            gx(k, own).wait_recv()
            gx(k, own, GXF).wait_recv()

    leaf = held.at[3 - 2 * core]
    weights = weights_of(both(leaf), both(hub))
    terms = to_texts(weights, both(hub))

    @pl.when(core == 0)
    def _():
        ret_x[...] = terms.astype(jnp.bfloat16).reshape(2, rows, width)

    @pl.when(core == 1)
    def _():
        total[2] += terms

    terms = to_images(weights, both(leaf))

    @pl.when(core == 0)
    def _():
        total[0] += terms

    @pl.when(core == 1)
    def _():
        ret_x[...] = (total[1] + terms).astype(jnp.bfloat16).reshape(2, rows, width)

    def rx(k, slot, kind):
        return remote(kind, k, ret_x.at[slot], got_x.at[slot], dev_from)

    def ra(k):
        return remote(RA_, k, ret_a, got_a, dev_a)

    def rb(k):
        return remote(RB_, k, ret_b, got_b, dev_b)

    for k in range(CHUNKS):
        rx(k, other, RXP).start()
    for k in range(CHUNKS):
        rx(k, own, RXO).start()

    def slot_rows(slot, k):
        return pl.ds(pl.multiple_of(slot * rows + k * part, 16), part)

    f32 = jnp.float32

    @pl.when(core == 0)
    def _():
        for k in range(CHUNKS):
            at = pl.ds(k * part, part)
            ret_a[at, :] = total[0, slot_rows(other, k), :].astype(jnp.bfloat16)
            ra(k).start()
        for k in range(CHUNKS):
            at = pl.ds(k * part, part)
            rs(k, own, RSP).wait_recv()
            rx(k, own, RXP).wait_recv()
            ret_b[at, :] = (
                total[2, slot_rows(other, k), :]
                + got_s[other, at, :].astype(f32) + got_x[other, at, :].astype(f32)
            ).astype(jnp.bfloat16)
            rb(k).start()

    @pl.when(core == 1)
    def _():
        for k in range(CHUNKS):
            at = pl.ds(k * part, part)
            rs(k, own, RSP).wait_recv()
            ret_b[at, :] = (
                total[2, slot_rows(other, k), :] + got_s[other, at, :].astype(f32)
            ).astype(jnp.bfloat16)
            rb(k).start()
        for k in range(CHUNKS):
            at = pl.ds(k * part, part)
            rx(k, own, RXP).wait_recv()
            ret_a[at, :] = (
                total[0, slot_rows(other, k), :] + got_x[other, at, :].astype(f32)
            ).astype(jnp.bfloat16)
            ra(k).start()

    def finish(which, k, extra):
        at = pl.ds(k * part, part)
        kept = total[2 * which, slot_rows(own, k), :]
        far = (got_a, got_b)[which][at, :].astype(f32)
        direction = kept + far + extra
        inv = inverse[which, at, 0:1]
        unit = raw[which, at, :].astype(f32) * inv
        along = jnp.sum(unit * direction, axis=1, keepdims=True)
        out = (image_out, text_out)[which]
        out[at, :] = (direction - unit * along) * inv

    for k in range(CHUNKS):
        at = pl.ds(k * part, part)
        rs(k, own, RSO).wait_recv()
        rx(k, own, RXO).wait_recv()
        ra(k).wait_recv()
        rb(k).wait_recv()
        from_x = got_x[own, at, :].astype(f32)
        is_odd = core == 1
        finish(0, k, jnp.where(is_odd, from_x, 0.0))
        finish(1, k, jnp.where(is_odd, 0.0, from_x) + got_s[own, at, :].astype(f32))

    for k in range(CHUNKS):
        ga(k, own).wait_send()
        gb(k, own).wait_send()
        gx(k, own).wait_send()
        gs(k, own).wait_send()
        gs(k, own, GSF).wait_send()
        gx(k, own, GXF).wait_send()
        rs(k, own, RSP).wait_send()
        rs(k, own, RSO).wait_send()
        rx(k, own, RXP).wait_send()
        rx(k, own, RXO).wait_send()
        ra(k).wait_send()
        rb(k).wait_send()


def hand_over(image_ref, text_ref, image_out, text_out, sem):
    stores = [
        pltpu.make_async_copy(image_ref, image_out, sem.at[0]),
        pltpu.make_async_copy(text_ref, text_out, sem.at[1]),
    ]
    for store in stores:
        store.start()
    for store in stores:
        store.wait()


def local(image_embeds, text_embeds, pair_text, similarity_scale, logit_bias):
    rows, width = image_embeds.shape
    any_space = pl.BlockSpec(memory_space=pl.ANY)
    bf16, f32 = jnp.bfloat16, jnp.float32
    hbm_space = pl.BlockSpec(memory_space=pltpu.HBM)
    vmem_space = pl.BlockSpec(memory_space=pltpu.VMEM)
    found = pl.pallas_call(
        kernel,
        out_shape=(pltpu.VMEM((rows, width), f32),) * 2,
        in_specs=[hbm_space] * 5,
        out_specs=(vmem_space, vmem_space),
        scratch_shapes=[
            pltpu.VMEM((2, rows, width), bf16),
            pltpu.VMEM((4, 2, rows, width), bf16),
            pltpu.VMEM((2, rows, width), bf16),
            pltpu.VMEM((2, rows, width), bf16),
            pltpu.VMEM((rows, width), bf16),
            pltpu.VMEM((rows, width), bf16),
            pltpu.VMEM((2, rows, width), bf16),
            pltpu.VMEM((2, rows, width), bf16),
            pltpu.VMEM((rows, width), bf16),
            pltpu.VMEM((rows, width), bf16),
            pltpu.VMEM((3, 2 * rows, width), f32),
            pltpu.VMEM((2, rows, 128), f32),
            pltpu.VMEM((4 * rows,), jnp.int32),
            pltpu.SMEM((2, 1, 1), f32),
            pltpu.SemaphoreType.DMA((12 * CHUNKS,)),
            pltpu.SemaphoreType.DMA((12 * CHUNKS,)),
            pltpu.SemaphoreType.DMA((5,)),
        ],
        compiler_params=pltpu.CompilerParams(collective_id=0, has_side_effects=True),
        name="pair_grads",
    )(
        image_embeds, text_embeds, pair_text,
        similarity_scale.reshape(1, 1),
        logit_bias.reshape(1, 1),
    )
    return pl.pallas_call(
        hand_over,
        out_shape=(jax.ShapeDtypeStruct((rows, width), f32),) * 2,
        in_specs=[vmem_space] * 2,
        out_specs=(any_space, any_space),
        scratch_shapes=[pltpu.SemaphoreType.DMA((2,))],
        name="hand_over",
    )(*(pltpu.with_memory_space_constraint(value, pltpu.VMEM) for value in found))


def solution(mesh):
    return jax.shard_map(
        local,
        mesh=mesh,
        in_specs=(P(("blk", "node"), None), P(("blk", "node"), None), P(), P(), P()),
        out_specs=(P(("blk", "node"), None), P(("blk", "node"), None)),
        check_vma=False,
    )
```

```python
import functools

import jax
import jax.numpy as jnp
from jax import lax
from jax.experimental import pallas as pl
from jax.experimental.pallas import tpu as pltpu
from jax.sharding import PartitionSpec as P

MESH = pl.DeviceIdType.MESH
CHUNKS = 5
GA, GB, GS, GX, GSF, GXF, RXP, RXO, RSP, RSO, RA_, RB_, GXA = range(13)


def kernel(
    image_ref, text_ref, pair_ref, scale_ref, bias_ref,
    image_out, text_out,
    raw, held, ret_x, ret_s, ret_a, ret_b, got_x, got_s, got_a, got_b,
    total, inverse, pairs, scalars,
    send_sem, recv_sem, local_sem, ready,
):
    rows, width = image_ref.shape
    part = rows // CHUNKS
    blk_count = lax.axis_size("blk")
    node_count = lax.axis_size("node")
    me = lax.axis_index("blk")
    y = lax.axis_index("node")
    core = lax.rem(me, 2)
    own = lax.rem(y, 2)
    other = 1 - own
    mate_a = y + 1 - 2 * own
    mate_b = lax.rem(y + node_count - 1 + 2 * own, node_count)
    sibling = me + 1 - 2 * core
    x_to = lax.rem(me + 4 * core - 2 + blk_count, blk_count)
    x_from = lax.rem(me - 4 * core + 2 + blk_count, blk_count)
    dev_a = (me, mate_a)
    dev_b = (me, mate_b)
    dev_s = (sibling, y)
    dev_to = (x_to, y)
    dev_from = (x_from, y)

    def is_head(b):
        return b < 2

    def is_tail(b):
        return b >= blk_count - 2

    def is_first(b, n):
        return jnp.logical_and(b == 0, n == 0)

    def both_true(p, q):
        return jnp.logical_and(p, q)

    no = jnp.logical_not
    head, tail = is_head(me), is_tail(me)
    peers = (dev_a, dev_b, dev_s, dev_to, dev_from)
    mirror = (0, 1, 2, 4, 3)
    peer_late = [
        jnp.logical_or(
            both_true(is_first(*peer), no(tail)), both_true(is_tail(peer[0]), head)
        )
        for peer in peers
    ]
    me_late = [
        jnp.logical_or(
            both_true(is_first(me, y), no(is_tail(peer[0]))), both_true(tail, is_head(peer[0]))
        )
        for peer in peers
    ]

    swap_to = jnp.logical_or(
        jnp.logical_and(me == 0, y != 3), jnp.logical_and(me == 2, y == 0)
    )
    swap_from = jnp.logical_or(
        jnp.logical_and(me == blk_count - 2, y != 3), is_first(me, y)
    )

    barrier = pltpu.get_barrier_semaphore()
    expected = 5
    for r, peer in enumerate(peers):
        @pl.when(no(me_late[r]))
        def _():
            pl.semaphore_signal(barrier, inc=1, device_id=peer, device_id_type=MESH)

        expected = expected - jnp.where(peer_late[r], 1, 0)

    load_image = pltpu.make_async_copy(image_ref, raw.at[0], local_sem.at[0])
    load_text = pltpu.make_async_copy(text_ref, raw.at[1], local_sem.at[1])
    load_pairs = pltpu.make_async_copy(
        pair_ref.at[pl.ds(pl.multiple_of(me * (rows * 4), 128), rows * 4)], pairs, local_sem.at[2]
    )
    load_scale = pltpu.make_async_copy(scale_ref, scalars.at[0], local_sem.at[3])
    load_bias = pltpu.make_async_copy(bias_ref, scalars.at[1], local_sem.at[4])
    for load in (load_image, load_text, load_pairs, load_scale, load_bias):
        load.start()

    def normalise(which):
        for k in range(5):
            at = pl.ds(k * (rows // 5), rows // 5)
            values = raw[which, at, :].astype(jnp.float32)
            inv = lax.rsqrt(jnp.sum(values * values, axis=1, keepdims=True) + 1e-06)
            inverse[which, at, :] = jnp.broadcast_to(inv, (rows // 5, 128))
            held[which, own, at, :] = (values * inv).astype(jnp.bfloat16)

    load_image.wait()
    normalise(0)
    load_text.wait()
    normalise(1)

    pl.semaphore_wait(barrier, expected)
    for r, peer in enumerate(peers):
        @pl.when(me_late[r])
        def _():
            pl.semaphore_signal(
                ready.at[mirror[r]], inc=1, device_id=peer, device_id_type=MESH
            )

    def remote(kind, k, src, dst, device, landing=None):
        landing = kind if landing is None else landing
        at = pl.ds(k * part, part)
        return pltpu.make_async_remote_copy(
            src_ref=src.at[at, :],
            dst_ref=dst.at[at, :],
            send_sem=send_sem.at[kind * CHUNKS + k],
            recv_sem=recv_sem.at[landing * CHUNKS + k],
            device_id=device,
            device_id_type=MESH,
        )

    def ga(k, slot):
        return remote(GA, k, held.at[0, slot], held.at[0, slot], dev_a)

    def gb(k, slot):
        return remote(GB, k, held.at[1, slot], held.at[1, slot], dev_b)

    def gs(k, slot, kind=GS):
        return remote(kind, k, held.at[1, slot], held.at[2, slot], dev_s)

    def gx(k, slot, kind=GX):
        return remote(kind, k, held.at[1 - core, slot], held.at[3, slot], dev_to)

    def ga_x(k):
        return remote(GXA, k, held.at[3, own], held.at[3, own], dev_a, GXF)

    def start_own(kind):
        for k in range(CHUNKS):
            kind(k, own).start()

    def late_sends(r, kind):
        @pl.when(peer_late[r])
        def _():
            pl.semaphore_wait(ready.at[r], 1)
            if kind is not None:
                start_own(kind)

    hold_a = both_true(tail, core == 1)
    for r, kind in ((3, gx), (0, ga), (1, gb), (2, gs)):
        wait_more = {3: swap_to, 0: hold_a}.get(r, False)

        @pl.when(no(jnp.logical_or(peer_late[r], wait_more)))
        def _():
            start_own(kind)

    @pl.when(hold_a)
    def _():
        for k in range(CHUNKS):
            gx(k, own).wait_send()
        start_own(ga)

    for r, kind in ((0, ga), (1, gb), (2, gs)):
        late_sends(r, kind)

    @pl.when(core == 0)
    def _():
        late_sends(3, None)

        @pl.when(both_true(peer_late[3], no(swap_to)))
        def _():
            start_own(gx)

    load_pairs.wait()
    load_scale.wait()
    load_bias.wait()
    scale = scalars[0, 0, 0]
    bias = scalars[1, 0, 0]

    def take_b():
        for k in range(CHUNKS):
            gb(k, own).wait_recv()

            @pl.when(core == 0)
            def _():
                gx(k, other, GXF).start()

            gs(k, other, GSF).start()

        @pl.when(swap_to)
        def _():
            start_own(gx)

    def take_a():
        for k in range(CHUNKS):
            ga(k, own).wait_recv()

            @pl.when(both_true(core == 1, no(tail)))
            def _():
                gx(k, other, GXF).start()

    def both(ref):
        return ref[...].reshape(2 * rows, width)

    def weights_of(texts, images, positive=None):
        logits = scale * lax.dot_general(
            texts, images, (((1,), (1,)), ((), ())), preferred_element_type=jnp.float32
        ) + bias
        if positive is None:
            return (scale * jax.nn.sigmoid(logits)).astype(jnp.bfloat16)
        sign = jnp.where(positive, 1.0, -1.0)
        return (-sign * scale * jax.nn.sigmoid(-sign * logits)).astype(jnp.bfloat16)

    def to_texts(weights, images):
        return jnp.dot(weights, images, preferred_element_type=jnp.float32)

    def to_images(weights, texts):
        return lax.dot_general(
            weights, texts, (((0,), (0,)), ((), ())), preferred_element_type=jnp.float32
        )

    wide = pairs[...].reshape(1, 4 * rows) - me * (4 * rows)
    target = jnp.where(y < 2, wide[:, : 2 * rows], wide[:, 2 * rows :])
    even_y = jnp.where(own == 0, y, mate_b)
    odd_y = jnp.where(own == 0, mate_b, y)
    row_id = lax.broadcasted_iota(jnp.int32, (2 * rows, 1), 0)
    text_id = jnp.where(row_id < rows, row_id + even_y * rows, row_id - rows + odd_y * rows)
    positive = text_id == target

    def own_pair(first):
        texts, images = both(held.at[1]), both(held.at[0])
        weights = weights_of(texts, images, positive)
        total[2] = to_texts(weights, images)
        if first:
            total[0] = to_images(weights, texts)
        else:
            total[0] += to_images(weights, texts)

    def wait_sibling():
        for k in range(CHUNKS):
            gs(k, own).wait_recv()
            gs(k, own, GSF).wait_recv()

    def rs(k, slot, kind):
        return remote(kind, k, ret_s.at[slot], got_s.at[slot], dev_s)

    def rx(k, slot, kind):
        return remote(kind, k, ret_x.at[slot], got_x.at[slot], dev_from)

    def ra(k):
        return remote(RA_, k, ret_a, got_a, dev_a)

    def rb(k):
        return remote(RB_, k, ret_b, got_b, dev_b)

    def slot_rows(slot, k):
        return pl.ds(pl.multiple_of(slot * rows + k * part, 16), part)

    f32 = jnp.float32

    bf16 = jnp.bfloat16
    slots = ((own, GX, RXO), (other, GXF, RXP))

    def return_a(extra):
        for k in range(CHUNKS):
            at = pl.ds(k * part, part)
            value = total[0, slot_rows(other, k), :]
            if extra:
                rx(k, own, RXP).wait_recv()
                value = value + got_x[other, at, :].astype(f32)
            ret_a[at, :] = value.astype(bf16)
            ra(k).start()

    def ready_from():
        @pl.when(peer_late[4])
        def _():
            pl.semaphore_wait(ready.at[4], 1)

    order = (
        (jnp.where(swap_from, other, own), jnp.where(swap_from, GXF, GX),
         jnp.where(swap_from, RXP, RXO)),
        (jnp.where(swap_from, own, other), jnp.where(swap_from, GX, GXF),
         jnp.where(swap_from, RXO, RXP)),
    )

    def remote_texts(turn):
        slot, kind, back = order[turn]
        for k in range(CHUNKS):
            gx(k, slot, kind).wait_recv()
        images, texts = both(held.at[0]), held[3, slot]
        weights = weights_of(texts, images)
        ret_x[slot] = to_texts(weights, images).astype(bf16)
        for k in range(CHUNKS):
            rx(k, slot, back).start()
        if turn == 0:
            total[0] = to_images(weights, texts)
        else:
            total[0] += to_images(weights, texts)

    @pl.when(core == 0)
    def _():
        @pl.when(tail)
        def _():
            take_a()
            remote_texts(0)
            take_b()

        @pl.when(no(tail))
        def _():
            take_b()
            take_a()
            ready_from()
            remote_texts(0)

        own_pair(False)
        remote_texts(1)
        wait_sibling()
        images, texts = both(held.at[0]), both(held.at[2])
        weights = weights_of(texts, images)
        ret_s[...] = to_texts(weights, images).astype(bf16).reshape(2, rows, width)
        for k in range(CHUNKS):
            rs(k, other, RSP).start()
        for k in range(CHUNKS):
            rs(k, own, RSO).start()
        total[0] += to_images(weights, texts)

        return_a(False)

        for k in range(CHUNKS):
            at = pl.ds(k * part, part)
            rs(k, own, RSP).wait_recv()
            rx(k, own, RXP).wait_recv()
            ret_b[at, :] = (
                total[2, slot_rows(other, k), :]
                + got_s[other, at, :].astype(f32) + got_x[other, at, :].astype(f32)
            ).astype(bf16)
            rb(k).start()

    @pl.when(core == 1)
    def _():
        take_a()
        take_b()
        own_pair(True)
        wait_sibling()
        ready_from()

        @pl.when(head)
        def _():
            for k in range(CHUNKS):
                gx(k, own).wait_recv()
                ga_x(k).start()

        texts = held[1:3].reshape(4 * rows, width)
        for slot, kind, back in slots:
            if kind == GX:
                @pl.when(no(head))
                def _():
                    for k in range(CHUNKS):
                        gx(k, slot, kind).wait_recv()
            else:
                @pl.when(head)
                def _():
                    return_a(True)

                for k in range(CHUNKS):
                    gx(k, slot, kind).wait_recv()
            images = held[3, slot]
            weights = weights_of(texts, images)
            ret_x[slot] = to_images(weights, texts).astype(bf16)
            for k in range(CHUNKS):
                rx(k, slot, back).start()
            terms = to_texts(weights, images)
            total[2] += terms[: 2 * rows]
            if kind == GX:
                total[1] = terms[2 * rows :]
            else:
                terms = total[1] + terms[2 * rows :]
                ret_s[...] = terms.astype(bf16).reshape(2, rows, width)
        for k in range(CHUNKS):
            rs(k, other, RSP).start()
        for k in range(CHUNKS):
            rs(k, own, RSO).start()

        for k in range(CHUNKS):
            at = pl.ds(k * part, part)
            rs(k, own, RSP).wait_recv()
            ret_b[at, :] = (
                total[2, slot_rows(other, k), :] + got_s[other, at, :].astype(f32)
            ).astype(bf16)
            rb(k).start()

        @pl.when(jnp.logical_not(head))
        def _():
            return_a(True)

    def finish(which, k, extra):
        at = pl.ds(k * part, part)
        kept = total[2 * which, slot_rows(own, k), :]
        far = (got_a, got_b)[which][at, :].astype(f32)
        direction = kept + far + extra
        inv = inverse[which, at, 0:1]
        unit = raw[which, at, :].astype(f32) * inv
        along = jnp.sum(unit * direction, axis=1, keepdims=True)
        out = (image_out, text_out)[which]
        out[at, :] = (direction - unit * along) * inv

    for k in range(CHUNKS):
        at = pl.ds(k * part, part)
        rs(k, own, RSO).wait_recv()
        rx(k, own, RXO).wait_recv()
        ra(k).wait_recv()
        rb(k).wait_recv()
        from_x = got_x[own, at, :].astype(f32)
        is_odd = core == 1
        finish(0, k, jnp.where(is_odd, from_x, 0.0))
        finish(1, k, jnp.where(is_odd, 0.0, from_x) + got_s[own, at, :].astype(f32))

    for k in range(CHUNKS):
        ga(k, own).wait_send()
        gb(k, own).wait_send()
        gs(k, own).wait_send()

        @pl.when(no(hold_a))
        def _():
            gx(k, own).wait_send()

        gs(k, own, GSF).wait_send()

        @pl.when(jnp.logical_or(core == 0, no(tail)))
        def _():
            gx(k, own, GXF).wait_send()

        @pl.when(jnp.logical_and(core == 1, head))
        def _():
            ga_x(k).wait_send()

        rs(k, own, RSP).wait_send()
        rs(k, own, RSO).wait_send()
        rx(k, own, RXP).wait_send()
        rx(k, own, RXO).wait_send()
        ra(k).wait_send()
        rb(k).wait_send()


def hand_over(image_ref, text_ref, image_out, text_out, sem):
    stores = [
        pltpu.make_async_copy(image_ref, image_out, sem.at[0]),
        pltpu.make_async_copy(text_ref, text_out, sem.at[1]),
    ]
    for store in stores:
        store.start()
    for store in stores:
        store.wait()


def local(image_embeds, text_embeds, pair_text, similarity_scale, logit_bias):
    rows, width = image_embeds.shape
    any_space = pl.BlockSpec(memory_space=pl.ANY)
    bf16, f32 = jnp.bfloat16, jnp.float32
    hbm_space = pl.BlockSpec(memory_space=pltpu.HBM)
    vmem_space = pl.BlockSpec(memory_space=pltpu.VMEM)
    found = pl.pallas_call(
        kernel,
        out_shape=(pltpu.VMEM((rows, width), f32),) * 2,
        in_specs=[hbm_space] * 5,
        out_specs=(vmem_space, vmem_space),
        scratch_shapes=[
            pltpu.VMEM((2, rows, width), bf16),
            pltpu.VMEM((4, 2, rows, width), bf16),
            pltpu.VMEM((2, rows, width), bf16),
            pltpu.VMEM((2, rows, width), bf16),
            pltpu.VMEM((rows, width), bf16),
            pltpu.VMEM((rows, width), bf16),
            pltpu.VMEM((2, rows, width), bf16),
            pltpu.VMEM((2, rows, width), bf16),
            pltpu.VMEM((rows, width), bf16),
            pltpu.VMEM((rows, width), bf16),
            pltpu.VMEM((3, 2 * rows, width), f32),
            pltpu.VMEM((2, rows, 128), f32),
            pltpu.VMEM((4 * rows,), jnp.int32),
            pltpu.SMEM((2, 1, 1), f32),
            pltpu.SemaphoreType.DMA((13 * CHUNKS,)),
            pltpu.SemaphoreType.DMA((13 * CHUNKS,)),
            pltpu.SemaphoreType.DMA((5,)),
            pltpu.SemaphoreType.REGULAR((5,)),
        ],
        compiler_params=pltpu.CompilerParams(collective_id=0, has_side_effects=True),
        name="pair_grads",
    )(
        image_embeds, text_embeds, pair_text,
        similarity_scale.reshape(1, 1),
        logit_bias.reshape(1, 1),
    )
    return pl.pallas_call(
        hand_over,
        out_shape=(jax.ShapeDtypeStruct((rows, width), f32),) * 2,
        in_specs=[vmem_space] * 2,
        out_specs=(any_space, any_space),
        scratch_shapes=[pltpu.SemaphoreType.DMA((2,))],
        name="hand_over",
    )(*(pltpu.with_memory_space_constraint(value, pltpu.VMEM) for value in found))


def solution(mesh):
    return jax.shard_map(
        local,
        mesh=mesh,
        in_specs=(P(("blk", "node"), None), P(("blk", "node"), None), P(), P(), P()),
        out_specs=(P(("blk", "node"), None), P(("blk", "node"), None)),
        check_vma=False,
    )
```

```python
import functools

import jax
import jax.numpy as jnp
from jax import lax
from jax.experimental import pallas as pl
from jax.experimental.pallas import tpu as pltpu
from jax.sharding import PartitionSpec as P

MESH = pl.DeviceIdType.MESH
CHUNKS = 5
PIECES = 1
GA, GB, GS, GX, GSF, GXF, RXP, RXO, RSP, RSO, RA_, RB_, GXA, GW, GWA = range(15)


def kernel(
    image_ref, text_ref, pair_ref, scale_ref, bias_ref,
    image_out, text_out,
    raw, held, ret_x, ret_s, ret_a, ret_b, got_x, got_s, got_a, got_b,
    total, inverse, pairs, scalars,
    send_sem, recv_sem, local_sem, ready,
):
    rows, width = image_ref.shape
    part = rows // CHUNKS
    blk_count = lax.axis_size("blk")
    node_count = lax.axis_size("node")
    me = lax.axis_index("blk")
    y = lax.axis_index("node")
    core = lax.rem(me, 2)
    own = lax.rem(y, 2)
    other = 1 - own
    mate_a = y + 1 - 2 * own
    mate_b = lax.rem(y + node_count - 1 + 2 * own, node_count)
    sibling = me + 1 - 2 * core
    x_to = lax.rem(me + 4 * core - 2 + blk_count, blk_count)
    x_from = lax.rem(me - 4 * core + 2 + blk_count, blk_count)
    dev_a = (me, mate_a)
    dev_b = (me, mate_b)
    dev_s = (sibling, y)
    dev_to = (x_to, y)
    dev_from = (x_from, y)

    def is_head(b):
        return b < 2

    def is_tail(b):
        return b >= blk_count - 2

    def is_first(b, n):
        return jnp.logical_and(b == 0, n == 0)

    def both_true(p, q):
        return jnp.logical_and(p, q)

    no = jnp.logical_not
    head, tail = is_head(me), is_tail(me)
    peers = (dev_a, dev_b, dev_s, dev_to, dev_from)
    mirror = (0, 1, 2, 4, 3)
    peer_late = [
        jnp.logical_or(
            both_true(is_first(*peer), no(tail)), both_true(is_tail(peer[0]), head)
        )
        for peer in peers
    ]
    me_late = [
        jnp.logical_or(
            both_true(is_first(me, y), no(is_tail(peer[0]))), both_true(tail, is_head(peer[0]))
        )
        for peer in peers
    ]

    swap_to = jnp.logical_and(me == 2, y == 0)
    swap_from = is_first(me, y)
    head_0 = both_true(head, core == 0)
    head_1 = both_true(head, core == 1)
    tail_0 = both_true(tail, core == 0)
    tail_1 = both_true(tail, core == 1)

    barrier = pltpu.get_barrier_semaphore()
    expected = 5
    for r, peer in enumerate(peers):
        @pl.when(no(me_late[r]))
        def _():
            pl.semaphore_signal(barrier, inc=1, device_id=peer, device_id_type=MESH)

        expected = expected - jnp.where(peer_late[r], 1, 0)

    load_image = pltpu.make_async_copy(image_ref, raw.at[0], local_sem.at[0])
    load_text = pltpu.make_async_copy(text_ref, raw.at[1], local_sem.at[1])
    load_pairs = pltpu.make_async_copy(
        pair_ref.at[pl.ds(pl.multiple_of(me * (rows * 4), 128), rows * 4)], pairs, local_sem.at[2]
    )
    load_scale = pltpu.make_async_copy(scale_ref, scalars.at[0], local_sem.at[3])
    load_bias = pltpu.make_async_copy(bias_ref, scalars.at[1], local_sem.at[4])
    for load in (load_image, load_text, load_pairs, load_scale, load_bias):
        load.start()

    def normalise(which):
        for k in range(5):
            at = pl.ds(k * (rows // 5), rows // 5)
            values = raw[which, at, :].astype(jnp.float32)
            inv = lax.rsqrt(jnp.sum(values * values, axis=1, keepdims=True) + 1e-06)
            inverse[which, at, :] = jnp.broadcast_to(inv, (rows // 5, 128))
            held[which, own, at, :] = (values * inv).astype(jnp.bfloat16)

    load_image.wait()
    normalise(0)
    load_text.wait()
    normalise(1)

    pl.semaphore_wait(barrier, expected)
    for r, peer in enumerate(peers):
        @pl.when(me_late[r])
        def _():
            pl.semaphore_signal(
                ready.at[mirror[r]], inc=1, device_id=peer, device_id_type=MESH
            )

    def remote(kind, k, src, dst, device, landing=None):
        landing = kind if landing is None else landing
        at = pl.ds(k * part, part)
        return pltpu.make_async_remote_copy(
            src_ref=src.at[at, :],
            dst_ref=dst.at[at, :],
            send_sem=send_sem.at[kind * CHUNKS + k],
            recv_sem=recv_sem.at[landing * CHUNKS + k],
            device_id=device,
            device_id_type=MESH,
        )

    def ga(k, slot):
        return remote(GA, k, held.at[0, slot], held.at[0, slot], dev_a)

    def gb(k, slot):
        return remote(GB, k, held.at[1, slot], held.at[1, slot], dev_b)

    def gs(k, slot, kind=GS):
        return remote(kind, k, held.at[1, slot], held.at[2, slot], dev_s)

    def gx(k, slot, kind=GX):
        return remote(kind, k, held.at[1 - core, slot], held.at[3, slot], dev_to)

    def ga_x(k):
        return remote(GXA, k, held.at[3, own], held.at[3, own], dev_a, GXF)

    def start_own(kind):
        for k in range(CHUNKS):
            kind(k, own).start()

    def late_sends(r, kind):
        @pl.when(peer_late[r])
        def _():
            pl.semaphore_wait(ready.at[r], 1)
            if kind is not None:
                start_own(kind)

    for r, kind in ((3, gx), (0, ga), (1, gb), (2, gs)):
        wait_more = {3: swap_to, 0: tail_1}.get(r, False)

        @pl.when(no(jnp.logical_or(peer_late[r], wait_more)))
        def _():
            start_own(kind)

    @pl.when(tail_1)
    def _():
        for k in range(CHUNKS):
            gx(k, own).wait_send()
        start_own(ga)

    def gw(k):
        return remote(GW, k, held.at[0, own], held.at[4, own], dev_from)

    def straight(n):
        return n >= 0

    def gw_x(k):
        return remote(GWA, k, held.at[0, other], held.at[4, other], dev_from)

    def gw_a(k):
        return remote(GWA, k, held.at[4, own], held.at[4, own], dev_a)

    @pl.when(tail_0)
    def _():
        for k in range(CHUNKS):
            ga(k, own).wait_send()
        start_own(lambda k, slot: gw(k))

    @pl.when(both_true(tail_0, straight(y)))
    def _():
        for k in range(CHUNKS):
            ga(k, own).wait_recv()
            gw_x(k).start()

    @pl.when(swap_to)
    def _():
        pl.semaphore_wait(ready.at[3], 1)

    load_pairs.wait()
    load_scale.wait()
    load_bias.wait()
    scale = scalars[0, 0, 0]
    bias = scalars[1, 0, 0]

    def take_b():
        for k in range(CHUNKS):
            gb(k, own).wait_recv()

            @pl.when(both_true(core == 0, no(head)))
            def _():
                gx(k, other, GXF).start()

            gs(k, other, GSF).start()

        @pl.when(swap_to)
        def _():
            for k in range(CHUNKS):
                gx(k, other, GXF).wait_send()
            start_own(gx)
            for k in range(CHUNKS):
                gx(k, own).wait_send()
            pl.semaphore_signal(ready.at[5], inc=1, device_id=dev_s, device_id_type=MESH)

    def take_a():
        for k in range(CHUNKS):
            @pl.when(no(both_true(tail_0, straight(y))))
            def _():
                ga(k, own).wait_recv()

            @pl.when(both_true(core == 1, no(tail)))
            def _():
                gx(k, other, GXF).start()

    @pl.when(head_0)
    def _():
        got_x[...] = jnp.zeros_like(got_x)

    def both(ref):
        return ref[...].reshape(2 * rows, width)

    def weights_of(texts, images, positive=None):
        logits = scale * lax.dot_general(
            texts, images, (((1,), (1,)), ((), ())), preferred_element_type=jnp.float32
        ) + bias
        if positive is None:
            return (scale * jax.nn.sigmoid(logits)).astype(jnp.bfloat16)
        sign = jnp.where(positive, 1.0, -1.0)
        return (-sign * scale * jax.nn.sigmoid(-sign * logits)).astype(jnp.bfloat16)

    def to_texts(weights, images):
        return jnp.dot(weights, images, preferred_element_type=jnp.float32)

    def to_images(weights, texts):
        return lax.dot_general(
            weights, texts, (((0,), (0,)), ((), ())), preferred_element_type=jnp.float32
        )

    wide = pairs[...].reshape(1, 4 * rows) - me * (4 * rows)
    target = jnp.where(y < 2, wide[:, : 2 * rows], wide[:, 2 * rows :])
    even_y = jnp.where(own == 0, y, mate_b)
    odd_y = jnp.where(own == 0, mate_b, y)
    row_id = lax.broadcasted_iota(jnp.int32, (2 * rows, 1), 0)
    text_id = jnp.where(row_id < rows, row_id + even_y * rows, row_id - rows + odd_y * rows)
    positive = text_id == target

    def own_pair(first):
        texts, images = both(held.at[1]), both(held.at[0])
        weights = weights_of(texts, images, positive)
        total[2] = to_texts(weights, images)
        if first:
            total[0] = to_images(weights, texts)
        else:
            total[0] += to_images(weights, texts)

    def wait_sibling():
        for k in range(CHUNKS):
            gs(k, own).wait_recv()
            gs(k, own, GSF).wait_recv()

    def rs(k, slot, kind):
        return remote(kind, k, ret_s.at[slot], got_s.at[slot], dev_s)

    def rx(k, slot, kind):
        return remote(kind, k, ret_x.at[slot], got_x.at[slot], dev_from)

    def ra(k):
        return remote(RA_, k, ret_a, got_a, dev_a)

    def rb(k):
        return remote(RB_, k, ret_b, got_b, dev_b)

    def slot_rows(slot, k):
        return pl.ds(pl.multiple_of(slot * rows + k * part, 16), part)

    f32 = jnp.float32

    bf16 = jnp.bfloat16
    slots = ((own, GX, RXO), (other, GXF, RXP))

    def return_a(extra):
        for k in range(CHUNKS):
            at = pl.ds(k * part, part)
            value = total[0, slot_rows(other, k), :]
            if extra:
                rx(k, own, RXP).wait_recv()
                value = value + got_x[other, at, :].astype(f32)
            ret_a[at, :] = value.astype(bf16)
            ra(k).start()

    def ready_from():
        @pl.when(peer_late[4])
        def _():
            pl.semaphore_wait(ready.at[4], 1)

    order = (
        (jnp.where(swap_from, other, own), jnp.where(swap_from, GXF, GX),
         jnp.where(swap_from, RXP, RXO)),
        (jnp.where(swap_from, own, other), jnp.where(swap_from, GX, GXF),
         jnp.where(swap_from, RXO, RXP)),
    )

    def remote_texts(turn):
        slot, kind, back = order[turn]
        for k in range(CHUNKS):
            gx(k, slot, kind).wait_recv()
        images, texts = both(held.at[0]), held[3, slot]
        weights = weights_of(texts, images)

        @pl.when(no(tail))
        def _():
            ret_x[slot] = to_texts(weights, images).astype(bf16)
            for k in range(CHUNKS):
                rx(k, slot, back).start()

        total[0] += to_images(weights, texts)

    def sibling_pair():
        wait_sibling()
        images, texts = both(held.at[0]), both(held.at[2])
        weights = weights_of(texts, images)
        ret_s[...] = to_texts(weights, images).astype(bf16).reshape(2, rows, width)
        for k in range(CHUNKS):
            rs(k, other, RSP).start()
        for k in range(CHUNKS):
            rs(k, own, RSO).start()
        total[0] += to_images(weights, texts)

    def return_b(extra):
        for k in range(CHUNKS):
            at = pl.ds(k * part, part)
            rs(k, own, RSP).wait_recv()
            value = total[2, slot_rows(other, k), :] + got_s[other, at, :].astype(f32)
            if extra:
                rx(k, own, RXP).wait_recv()
                value = value + got_x[other, at, :].astype(f32)
            ret_b[at, :] = value.astype(bf16)
            rb(k).start()

    @pl.when(core == 0)
    def _():
        late_sends(1, gb)
        take_b()
        late_sends(0, ga)

        @pl.when(head)
        def _():
            pl.semaphore_wait(ready.at[3], 1)
            start_own(gx)
            for k in range(CHUNKS):
                gx(k, other, GXF).start()

        take_a()
        ready_from()
        total[0] = jnp.zeros_like(total[0])
        first = is_first(me, y)

        @pl.when(first)
        def _():
            sibling_pair()

        remote_texts(0)
        own_pair(False)
        remote_texts(1)

        @pl.when(no(first))
        def _():
            sibling_pair()

        @pl.when(head)
        def _():
            for k in range(CHUNKS):
                gw(k).wait_recv()

                @pl.when(no(straight(mate_a)))
                def _():
                    gw_a(k).start()

            return_a(False)
            texts = both(held.at[1])
            for slot in (own, other):
                if slot is other:
                    for k in range(CHUNKS):
                        gw_a(k).wait_recv()
                images = held[4, slot]
                total[2] += to_texts(weights_of(texts, images), images)
            return_b(False)

        @pl.when(no(head))
        def _():
            return_a(False)
            return_b(True)

    @pl.when(core == 1)
    def _():
        take_a()
        late_sends(2, gs)
        take_b()
        own_pair(True)
        wait_sibling()
        ready_from()

        texts = held[1:3].reshape(4 * rows, width)

        def keep_terms(terms, kind):
            total[2] += terms[: 2 * rows]
            if kind == GX:
                total[1] = terms[2 * rows :]
            else:
                total[1] += terms[2 * rows :]

        def give_images(weights, slot, back):
            ret_x[slot] = to_images(weights, texts).astype(bf16)
            if back == RXO:
                @pl.when(both_true(me == 3, y == 0))
                def _():
                    pl.semaphore_wait(ready.at[5], 1)

            for k in range(CHUNKS):
                rx(k, slot, back).start()

        def give_sibling():
            ret_s[...] = total[1].astype(bf16).reshape(2, rows, width)
            for k in range(CHUNKS):
                rs(k, other, RSP).start()
            for k in range(CHUNKS):
                rs(k, own, RSO).start()

        @pl.when(head)
        def _():
            for k in range(CHUNKS):
                gx(k, own).wait_recv()
                ga_x(k).start()
            for slot, kind, back in slots:
                if kind != GX:
                    for k in range(CHUNKS):
                        gx(k, slot, kind).wait_recv()
                images = held[3, slot]
                weights = weights_of(texts, images)
                keep_terms(to_texts(weights, images), kind)
                if kind == GX:
                    give_images(weights, slot, back)
            return_b(False)
            give_sibling()
            give_images(weights, other, RXP)

        @pl.when(no(head))
        def _():
            for slot, kind, back in slots:
                for k in range(CHUNKS):
                    gx(k, slot, kind).wait_recv()
                images = held[3, slot]
                weights = weights_of(texts, images)
                give_images(weights, slot, back)
                keep_terms(to_texts(weights, images), kind)
            give_sibling()
            return_b(False)

        return_a(True)

    def finish(which, k, extra):
        at = pl.ds(k * part, part)
        kept = total[2 * which, slot_rows(own, k), :]
        far = (got_a, got_b)[which][at, :].astype(f32)
        direction = kept + far + extra
        inv = inverse[which, at, 0:1]
        unit = raw[which, at, :].astype(f32) * inv
        along = jnp.sum(unit * direction, axis=1, keepdims=True)
        out = (image_out, text_out)[which]
        out[at, :] = (direction - unit * along) * inv

    for k in range(CHUNKS):
        at = pl.ds(k * part, part)
        rs(k, own, RSO).wait_recv()

        @pl.when(no(head_0))
        def _():
            rx(k, own, RXO).wait_recv()

        ra(k).wait_recv()
        rb(k).wait_recv()
        from_x = got_x[own, at, :].astype(f32)
        is_odd = core == 1
        finish(0, k, jnp.where(is_odd, from_x, 0.0))
        finish(1, k, jnp.where(is_odd, 0.0, from_x) + got_s[own, at, :].astype(f32))

    def drained(condition, *copies):
        @pl.when(condition)
        def _():
            for copy in copies:
                copy.wait_send()

    for k in range(CHUNKS):
        for copy in (
            gb(k, own), gs(k, own), gs(k, own, GSF), rs(k, own, RSP), rs(k, own, RSO), ra(k), rb(k)
        ):
            copy.wait_send()
        drained(no(tail_0), ga(k, own), rx(k, own, RXP), rx(k, own, RXO))
        drained(no(jnp.logical_or(swap_to, tail_1)), gx(k, own), gx(k, own, GXF))
        drained(both_true(head_0, no(straight(mate_a))), gw_a(k))
        drained(tail_0, gw(k))
        drained(both_true(tail_0, straight(y)), gw_x(k))
        drained(head_1, ga_x(k))


def hand_over(image_ref, text_ref, image_out, text_out, sem):
    part = image_ref.shape[0] // PIECES
    stores = []
    for k in range(PIECES):
        at = pl.ds(k * part, part)
        for which, (src, dst) in enumerate(((image_ref, image_out), (text_ref, text_out))):
            stores.append(
                pltpu.make_async_copy(src.at[at, :], dst.at[at, :], sem.at[2 * k + which])
            )
            stores[-1].start()
    for store in stores:
        store.wait()


def local(image_embeds, text_embeds, pair_text, similarity_scale, logit_bias):
    rows, width = image_embeds.shape
    any_space = pl.BlockSpec(memory_space=pl.ANY)
    bf16, f32 = jnp.bfloat16, jnp.float32
    hbm_space = pl.BlockSpec(memory_space=pltpu.HBM)
    vmem_space = pl.BlockSpec(memory_space=pltpu.VMEM)
    found = pl.pallas_call(
        kernel,
        out_shape=(pltpu.VMEM((rows, width), f32),) * 2,
        in_specs=[hbm_space] * 5,
        out_specs=(vmem_space, vmem_space),
        scratch_shapes=[
            pltpu.VMEM((2, rows, width), bf16),
            pltpu.VMEM((5, 2, rows, width), bf16),
            pltpu.VMEM((2, rows, width), bf16),
            pltpu.VMEM((2, rows, width), bf16),
            pltpu.VMEM((rows, width), bf16),
            pltpu.VMEM((rows, width), bf16),
            pltpu.VMEM((2, rows, width), bf16),
            pltpu.VMEM((2, rows, width), bf16),
            pltpu.VMEM((rows, width), bf16),
            pltpu.VMEM((rows, width), bf16),
            pltpu.VMEM((3, 2 * rows, width), f32),
            pltpu.VMEM((2, rows, 128), f32),
            pltpu.VMEM((4 * rows,), jnp.int32),
            pltpu.SMEM((2, 1, 1), f32),
            pltpu.SemaphoreType.DMA((15 * CHUNKS,)),
            pltpu.SemaphoreType.DMA((15 * CHUNKS,)),
            pltpu.SemaphoreType.DMA((5,)),
            pltpu.SemaphoreType.REGULAR((6,)),
        ],
        compiler_params=pltpu.CompilerParams(collective_id=0, has_side_effects=True),
        name="pair_grads",
    )(
        image_embeds, text_embeds, pair_text,
        similarity_scale.reshape(1, 1),
        logit_bias.reshape(1, 1),
    )
    return pl.pallas_call(
        hand_over,
        out_shape=(jax.ShapeDtypeStruct((rows, width), f32),) * 2,
        in_specs=[vmem_space] * 2,
        out_specs=(any_space, any_space),
        scratch_shapes=[pltpu.SemaphoreType.DMA((2 * PIECES,))],
        name="hand_over",
    )(*(pltpu.with_memory_space_constraint(value, pltpu.VMEM) for value in found))


def solution(mesh):
    return jax.shard_map(
        local,
        mesh=mesh,
        in_specs=(P(("blk", "node"), None), P(("blk", "node"), None), P(), P(), P()),
        out_specs=(P(("blk", "node"), None), P(("blk", "node"), None)),
        check_vma=False,
    )
```
